128 devices in a mesh: rep: 32 (over x, y, core), grp: 4 (over z).
Axes of the slice: x: 4, y: 4, z: 4, core: 2. Of those that a mesh axis runs over, the one named last changes fastest.
Arguments:
- grads: bfloat16 [128, 2, 320, 2048], P(('rep', 'grp')), may hold values from -6 to 6
- errors: float32 [128, 2, 320, 2048], P(('rep', 'grp')), may hold values from -4 to 4
- warm_start: float32 [2, 32, 2048], replicated, may hold values from -0.125 to 0.125
- vec_grads: float32 [128, 2, 2048], P(('rep', 'grp')), may hold values from -6 to 6
- owners: int32 [12], replicated, may hold values from 0 to 127, as said below
- mat_momentum: float32 [256, 64, 2048], P(('rep', 'grp')), may hold values from -0.3 to 0.3
- mat_weights: float32 [256, 64, 2048], P(('rep', 'grp')), may hold values from -0.3 to 0.3
- vec_momentum: float32 [256, 2048], P(('rep', 'grp')), may hold values from -0.3 to 0.3
- vec_weights: float32 [256, 2048], P(('rep', 'grp')), may hold values from 0.5 to 1.5
Outputs:
- new_errors: float32 [128, 2, 320, 2048], P(('rep', 'grp'))
- mat_momentum_out: float32 [256, 64, 2048], P(('rep', 'grp'))
- mat_weights_out: float32 [256, 64, 2048], P(('rep', 'grp'))
- vec_momentum_out: float32 [256, 2048], P(('rep', 'grp'))
- vec_weights_out: float32 [256, 2048], P(('rep', 'grp'))
The draws below stay inside these ranges and needn't reach their ends.
Inputs may be any that keep to these rules, and one draw needn't show every extreme that they name: `owners`: no replica owns more than 2 items, and some replica owns exactly 2. Replicas 0 and 127 each own at least one item.
All inputs are finite; a program needn't handle non-finite values.
Results may differ from the reference program's by a relative error of at most 0.0003.
Values sent between devices are 32-bit elements; how exact they have to be, the bound alone decides.
A program may use at most 64 MiB of HBM per device.

```python
import jax
import jax.numpy as jnp
from jax import lax

D = 2048
KVH = 5
HD = 64
R = 32
SLOTS = 2
ROOT_ITERS = 12
KVW = 320
REPLICAS = 128
NITEM = 12


def draw_owners(key, part):
    key_perm, key_pick, key_order = jax.random.split(key, 3)
    middle = jax.random.permutation(key_perm, REPLICAS - 2)[:NITEM - 3] + 1
    ends = jnp.array([0, REPLICAS - 1], dtype=jnp.int32)
    devices = jnp.concatenate([ends, middle.astype(jnp.int32)])
    extra = devices[jax.random.randint(key_pick, (), 0, NITEM - 1)]
    full = jnp.concatenate([devices, extra[None]])
    order = jax.random.permutation(key_order, NITEM)
    return full[order].astype(jnp.int32)


def levels(rng, extent, pieces, least, largest):
    factor_of, own = 1.0, jax.random.fold_in(rng, 6)
    for position, parts in pieces:
        heights = jnp.exp(jax.random.uniform(jax.random.fold_in(own, position), (parts,), jnp.float32, least / len(pieces), largest / len(pieces)))
        factor_of = factor_of * jnp.repeat(heights, extent[position] // parts).reshape([-1 if axis == position else 1 for axis in range(len(extent))])
    return factor_of


def normal_values(key, dims, scale, bound, shards=(), kind=jnp.bfloat16):
    drawn = jax.random.normal(key, dims, jnp.float32) * scale
    if len(shards) > 0:
        drawn = levels(key, dims, shards, -0.22, 0.18) * drawn
    return jnp.clip(drawn, min=-bound, max=bound).astype(kind)


def setup_inputs(seed: int = 0) -> dict:
    key_list = jax.random.split(jax.random.key(seed), 10)
    return {
        "grads": normal_values(key_list[0], (REPLICAS, 2, KVW, D), 1.0, 6.0, ((0, 128),)),
        "errors": normal_values(key_list[1], (REPLICAS, 2, KVW, D), 0.5, 4.0, ((0, 128),), jnp.float32),
        "warm_start": normal_values(key_list[2], (2, R, D), D ** -0.5, 0.125, (), jnp.float32),
        "vec_grads": normal_values(key_list[3], (REPLICAS, 2, D), 1.0, 6.0, ((0, 128),), jnp.float32),
        "owners": draw_owners(jax.random.fold_in(key_list[9], 71), 0),
        "mat_momentum": normal_values(key_list[5], (REPLICAS * SLOTS, HD, D), 0.05, 0.3, ((0, 128),), jnp.float32),
        "mat_weights": normal_values(key_list[6], (REPLICAS * SLOTS, HD, D), 0.05, 0.3, ((0, 128),), jnp.float32),
        "vec_momentum": normal_values(key_list[7], (REPLICAS * SLOTS, D), 0.05, 0.3, ((0, 128),), jnp.float32),
        "vec_weights": jnp.clip(1.0 + 0.1 * jax.random.normal(key_list[8], (REPLICAS * SLOTS, D), jnp.float32), 0.5, 1.5),
    }


high = lax.Precision.HIGHEST

def orthonormal(factor):
    gram_matrix = jnp.einsum('mkr,mks->mrs', factor, factor, precision=high)
    spread = jnp.sqrt(lax.optimization_barrier(jnp.sum(gram_matrix * gram_matrix, axis=(1, 2))))[:, None, None]
    identity_mat = jnp.broadcast_to(jnp.eye(gram_matrix.shape[1], dtype=jnp.float32), gram_matrix.shape).astype(gram_matrix.dtype)
    root_left = gram_matrix / spread
    root_right = identity_mat
    for sweep in range(ROOT_ITERS):
        middle = 1.5 * identity_mat - 0.5 * jnp.einsum('mrs,mst->mrt', root_right, root_left, precision=high)
        root_left = jnp.einsum('mrs,mst->mrt', root_left, middle, precision=high)
        root_right = jnp.einsum('mrs,mst->mrt', middle, root_right, precision=high)
    return jnp.einsum('mkr,mrs->mks', factor, root_right, precision=high) / jnp.sqrt(spread)

def replica_sum(term, grads, errors, init):

    def step(carry, pair):
        combined = pair[0].astype(jnp.float32) + pair[1]
        return (carry + term(combined), None)
    total, unused = lax.scan(step, init, (grads, errors))
    return total

def reference(grads, errors, warm_start, vec_grads, owners, mat_momentum, mat_weights, vec_momentum, vec_weights):
    q_factor = warm_start
    p_hat = None
    for round_index in range(2):
        p_sum = replica_sum(lambda c: jnp.einsum('mkd,mrd->mkr', c, q_factor, precision=high), grads, errors, jnp.zeros((2, KVW, R), jnp.float32))
        p_hat = orthonormal(p_sum / REPLICAS)
        q_sum = replica_sum(lambda c: jnp.einsum('mks,mkd->msd', p_hat, c, precision=high), grads, errors, jnp.zeros((2, R, D), jnp.float32))
        q_factor = q_sum / REPLICAS
    approx = jnp.einsum('mks,msd->mkd', p_hat, q_factor, precision=high)
    new_errors = lax.map(lambda pair: pair[0].astype(jnp.float32) + pair[1] - approx, (grads, errors))
    vec_avg = lax.optimization_barrier(jnp.sum(vec_grads, axis=0)) / REPLICAS
    earlier = jnp.arange(NITEM)[None, :] < jnp.arange(NITEM)[:, None]
    same = owners[None, :] == owners[:, None]
    slot = lax.optimization_barrier(jnp.sum((earlier & same).astype(jnp.int32), axis=1)).astype(jnp.int32)
    rows = (owners * SLOTS + slot).astype(jnp.int32)
    blocks = approx.reshape(2 * KVH, HD, D)
    for item in range(NITEM):
        where = rows[item]
        if item < 2 * KVH:
            moment = 0.9 * mat_momentum[where] + blocks[item]
            mat_momentum = mat_momentum.at[where].set(moment)
            mat_weights = mat_weights.at[where].set(mat_weights[where] - 0.5 * moment)
        else:
            moment = 0.9 * vec_momentum[where] + vec_avg[item - 2 * KVH]
            vec_momentum = vec_momentum.at[where].set(moment)
            vec_weights = vec_weights.at[where].set(vec_weights[where] - 0.5 * moment)
    return (new_errors, mat_momentum, mat_weights, vec_momentum, vec_weights)
```

```python
import functools

import jax
import jax.numpy as jnp
from jax import lax
from jax.experimental import pallas as pl
from jax.experimental.pallas import tpu as pltpu
from jax.sharding import PartitionSpec as P

ROOT_ITERS = 12
MESH = pl.DeviceIdType.MESH
HIGH = lax.Precision.HIGHEST
PARTS = 6
SPLITS = 4
SUBS = (32, 24)
STEPS = 2 * SPLITS + 2
CHUNK = 64


def dot(a, b, dims=((1,), (0,))):
    return lax.dot_general(a, b, (dims, ((), ())), precision=HIGH, preferred_element_type=jnp.float32)


def orthonormal(factor):
    rank = factor.shape[0]
    gram = dot(factor, factor, ((1,), (1,)))
    spread = jnp.sqrt(jnp.sum(gram * gram, keepdims=True))
    row = lax.broadcasted_iota(jnp.int32, (rank, rank), 0)
    column = lax.broadcasted_iota(jnp.int32, (rank, rank), 1)
    identity = jnp.where(row == column, 1.0, 0.0).astype(jnp.float32)
    left = gram / spread
    middle = 1.5 * identity - 0.5 * left
    left = dot(left, middle)
    right = middle
    for sweep in range(1, ROOT_ITERS):
        middle = 1.5 * identity - 0.5 * dot(right, left)
        if sweep < ROOT_ITERS - 1:
            left = dot(left, middle)
        right = dot(middle, right)
    return dot(right, factor, ((0,), (0,))) / jnp.sqrt(spread)


def reduce_kernel(grads_ref, errors_ref, warm_ref, vec_ref, q_out, p_out, v_out, *scratch):
    halves = scratch[:SPLITS]
    (
        grads, errors, away, pair, mine, whole0, whole1, middle, total, p_sums, p_recv, q_mine, q_pair, p_mine, p_pair,
        v_pair, load_sem, pair_sem, step_send, step_recv, p_sem, last_sem,
    ) = scratch[SPLITS:]
    core = lax.axis_index("rep") % 2
    place = (lax.axis_index("rep") // 8, (lax.axis_index("rep") // 2) % 4, lax.axis_index("grp"))
    rows, width = errors_ref.shape[2], errors_ref.shape[3]
    high = mine.shape[0]
    tail = high - rows
    count = lax.axis_size("rep") * lax.axis_size("grp")

    def device(x, y, z, c):
        return ((x * 4 + y) * 2 + c, z)

    bits, peers = [], []
    for kind in range(2):
        for axis in range(3):
            at = place[axis]
            moved = list(place)
            moved[axis] = at + 1 - 2 * (at % 2) if kind == 0 else 3 - at
            peers.append(device(*moved, core))
            bits.append((at + at // 2) % 2 if kind == 0 else at // 2)
    partner = device(*place, 1 - core)

    def remote(src, dst, send_sem, recv_sem, to):
        copy = pltpu.make_async_remote_copy(
            src_ref=src, dst_ref=dst, send_sem=send_sem, recv_sem=recv_sem, device_id=to, device_id_type=MESH
        )
        copy.start()
        return copy

    loads = {}
    starts = list(range(0, rows, CHUNK))
    for turn in range(2):
        matrix = 1 - core if turn == 0 else core
        for number, start in enumerate(starts):
            window = pl.ds(start, CHUNK)
            slot = turn * len(starts) + number
            loads[turn, number] = (
                pltpu.make_async_copy(grads_ref.at[0, matrix, window], grads.at[turn, window], load_sem.at[0, slot]),
                pltpu.make_async_copy(errors_ref.at[0, matrix, window], errors.at[turn, window], load_sem.at[1, slot]),
            )
            for copy in loads[turn, number]:
                copy.start()

    barrier = pltpu.get_barrier_semaphore()
    for peer in peers + [partner]:
        pl.semaphore_signal(barrier, inc=1, device_id=peer, device_id_type=MESH)

    first_row = lax.broadcasted_iota(jnp.int32, (tail, width), 0) == 0
    away[rows:, :] = jnp.where(first_row, vec_ref[0, pl.ds(1 - core, 1), :], 0.0)
    mine[rows:, :] = jnp.where(first_row, vec_ref[0, pl.ds(core, 1), :], 0.0)
    pl.semaphore_wait(barrier, len(peers) + 1)

    def combine(turn, number, into):
        for copy in loads[turn, number]:
            copy.wait()
        window = pl.ds(starts[number], CHUNK)
        into[window, :] = grads[turn, window, :].astype(jnp.float32) + errors[turn, window, :]

    sent = []
    handed = []
    for number, start in enumerate(starts):
        combine(0, number, away)
        window = pl.ds(start, CHUNK if number < len(starts) - 1 else CHUNK + tail)
        copy = remote(away.at[window], pair.at[window], pair_sem.at[0, number], pair_sem.at[1, number], partner)
        handed.append(copy)
        sent.append(copy)

    pieces = []
    for sub, size in enumerate(SUBS):
        for part in range(PARTS):
            pieces.append((part, PARTS * sum(SUBS[:sub]) + part * size, size))
    offsets = []
    for part in range(PARTS):
        chain = [0]
        for step in range(SPLITS):
            chain.append(chain[-1] + bits[(part + step) % 6] * (width >> (step + 1)))
        offsets.append(chain)

    def columns(part, depth):
        return pl.ds(pl.multiple_of(offsets[part][depth], 128), width >> depth)

    def others(part, depth):
        half = width >> depth
        begin = offsets[part][depth - 1] + (1 - bits[(part + depth - 1) % 6]) * half
        return pl.ds(pl.multiple_of(begin, 128), half)

    flight = {}

    def begin(step, number):
        part, start, size = pieces[number]
        window = pl.ds(start, size)
        link = (part + (step if step < SPLITS + 2 else STEPS - 1 - step)) % 6
        if step < SPLITS:
            src, dst = mine.at[window, others(part, step + 1)], halves[step].at[window]
        elif step == SPLITS:
            src, dst = mine.at[window, columns(part, SPLITS)], whole0.at[window]
        elif step == SPLITS + 1:
            src, dst = middle.at[window], whole1.at[window]
        else:
            src = dst = total.at[window, columns(part, STEPS - step)]
        flight[step, number] = remote(
            src, dst, step_send.at[step, number], step_recv.at[step, number], peers[link]
        )
        sent.append(flight[step, number])

    def finish(step, number):
        part, start, size = pieces[number]
        window = pl.ds(start, size)
        flight[step, number].wait_recv()
        if step < SPLITS:
            cols = columns(part, step + 1)
            mine[window, cols] = mine[window, cols] + halves[step][window, :]
        elif step == SPLITS:
            middle[window, :] = mine[window, columns(part, SPLITS)] + whole0[window, :]
        elif step == SPLITS + 1:
            total[window, columns(part, SPLITS)] = middle[window, :] + whole1[window, :]

    for number in range(len(starts)):
        combine(1, number, mine)
    for number, start in enumerate(starts):
        handed[number].wait_recv()
        size = CHUNK if number < len(starts) - 1 else CHUNK + tail
        window = pl.ds(start, size)
        mine[window, :] = mine[window, :] + pair[window, :]
        for piece, (part, first, extent) in enumerate(pieces):
            if start < first + extent <= start + size:
                begin(0, piece)

    rank = warm_ref.shape[1]
    live = lax.broadcasted_iota(jnp.int32, (rank, high), 1) < rows
    p_sums[0] = jnp.where(live, dot(warm_ref[core], mine[...], ((1,), (1,))), 0.0)
    p_flight = None
    for step in range(STEPS):
        if step < 6:
            p_flight = remote(p_sums.at[step], p_recv.at[step], p_sem.at[0, step], p_sem.at[1, step], peers[step])
            sent.append(p_flight)
        for number in range(len(pieces)):
            finish(step, number)
            if step < STEPS - 1:
                begin(step + 1, number)
        if step < 6:
            p_flight.wait_recv()
            p_sums[step + 1] = p_sums[step] + p_recv[step]
        if step == STEPS - 2:
            p_hat = orthonormal(p_sums[6] / count)
    v_copy = remote(total.at[pl.ds(rows, 8)], v_pair, last_sem.at[0, 0], last_sem.at[1, 0], partner)
    q_factor = dot(p_hat, total[...]) / count
    p_sum = jnp.where(live, dot(q_factor, total[...], ((1,), (1,))), 0.0)
    p_hat = orthonormal(p_sum / count)
    p_mine[...] = p_hat
    p_copy = remote(p_mine, p_pair, last_sem.at[0, 1], last_sem.at[1, 1], partner)
    q_mine[...] = dot(p_hat, total[...]) / count
    q_copy = remote(q_mine, q_pair, last_sem.at[0, 2], last_sem.at[1, 2], partner)
    v_out[core] = total[rows : rows + 8, :] / count
    p_out[core] = p_mine[...].T[:rows]
    q_out[core] = q_mine[...]
    v_copy.wait_recv()
    v_out[1 - core] = v_pair[...] / count
    p_copy.wait_recv()
    p_out[1 - core] = p_pair[...].T[:rows]
    q_copy.wait_recv()
    q_out[1 - core] = q_pair[...]
    for copy in sent + [v_copy, p_copy, q_copy]:
        copy.wait_send()


def apply_kernel(
    owners, grads, errors, p_hat, q_factor, vec_avg, mat_m, mat_w, vec_m, vec_w,
    new_errors, mat_m_out, mat_w_out, vec_m_out, vec_w_out,
):
    step = pl.program_id(0)
    device = lax.axis_index("rep") * lax.axis_size("grp") + lax.axis_index("grp")
    items = owners.shape[0]
    heads = items - vec_m.shape[0]

    def home(item):
        owner = owners[item]
        slot = jnp.int32(0)
        for before in range(items):
            slot += jnp.where((before < item) & (owners[before] == owner), 1, 0)
        return owner == device, slot

    @pl.when(step == 0)
    def _():
        mat_m_out[...] = mat_m[...]
        mat_w_out[...] = mat_w[...]
        vec_m_out[...] = vec_m[...]
        vec_w_out[...] = vec_w[...]
        for gain in range(items - heads):
            here, slot = home(heads + gain)

            @pl.when(here)
            def _():
                moment = 0.9 * vec_m[pl.ds(slot, 1), :] + vec_avg[gain, :1, :]
                vec_m_out[pl.ds(slot, 1), :] = moment
                vec_w_out[pl.ds(slot, 1), :] = vec_w[pl.ds(slot, 1), :] - 0.5 * moment

    approx = dot(p_hat[0], q_factor[0])
    new_errors[0, 0] = grads[0, 0].astype(jnp.float32) + errors[0, 0] - approx
    here, slot = home(step)

    @pl.when(here)
    def _():
        moment = 0.9 * mat_m[slot] + approx
        mat_m_out[slot] = moment
        mat_w_out[slot] = mat_w[slot] - 0.5 * moment


def local(grads, errors, warm_start, vec_grads, owners, mat_momentum, mat_weights, vec_momentum, vec_weights):
    _, matrices, rows, width = errors.shape
    rank = warm_start.shape[1]
    high = PARTS * sum(SUBS)
    f32 = jnp.float32
    pieces = PARTS * len(SUBS)
    vmem = pl.BlockSpec(memory_space=pltpu.VMEM)
    hbm = pl.BlockSpec(memory_space=pl.ANY)
    dma = pltpu.SemaphoreType.DMA
    q_factor, p_hat, vec_avg = pl.pallas_call(
        reduce_kernel,
        out_shape=(
            jax.ShapeDtypeStruct((matrices, rank, width), f32),
            jax.ShapeDtypeStruct((matrices, rows, rank), f32),
            jax.ShapeDtypeStruct((matrices, 8, width), f32),
        ),
        in_specs=[hbm, hbm, vmem, vmem],
        out_specs=(vmem, vmem, vmem),
        scratch_shapes=[pltpu.VMEM((high, width >> (step + 1)), f32) for step in range(SPLITS)]
        + [
            pltpu.VMEM((2, rows, width), jnp.bfloat16),
            pltpu.VMEM((2, rows, width), f32),
            pltpu.VMEM((high, width), f32),
            pltpu.VMEM((high, width), f32),
            pltpu.VMEM((high, width), f32),
            pltpu.VMEM((high, width >> SPLITS), f32),
            pltpu.VMEM((high, width >> SPLITS), f32),
            pltpu.VMEM((high, width >> SPLITS), f32),
            pltpu.VMEM((high, width), f32),
            pltpu.VMEM((7, rank, high), f32),
            pltpu.VMEM((6, rank, high), f32),
            pltpu.VMEM((rank, width), f32),
            pltpu.VMEM((rank, width), f32),
            pltpu.VMEM((rank, high), f32),
            pltpu.VMEM((rank, high), f32),
            pltpu.VMEM((8, width), f32),
            dma((2, 2 * (rows // CHUNK))),
            dma((2, rows // CHUNK)),
            dma((STEPS, pieces)),
            dma((STEPS, pieces)),
            dma((2, 6)),
            dma((2, 3)),
        ],
        compiler_params=pltpu.CompilerParams(
            collective_id=0, has_side_effects=True, vmem_limit_bytes=60 * 1024 * 1024
        ),
        name="reduce",
    )(grads, errors, warm_start, vec_grads)

    heads = rows // mat_momentum.shape[1]
    head = mat_momentum.shape[1]
    slots = mat_momentum.shape[0]
    block = pl.BlockSpec((1, 1, head, width), lambda i, owners: (0, i // heads, i % heads, 0))

    def fixed(*shape):
        return pl.BlockSpec(shape, lambda i, owners: (0,) * len(shape))

    mats, vecs = fixed(slots, head, width), fixed(slots, width)
    return pl.pallas_call(
        apply_kernel,
        out_shape=(
            jax.ShapeDtypeStruct(errors.shape, f32),
            jax.ShapeDtypeStruct(mat_momentum.shape, f32),
            jax.ShapeDtypeStruct(mat_weights.shape, f32),
            jax.ShapeDtypeStruct(vec_momentum.shape, f32),
            jax.ShapeDtypeStruct(vec_weights.shape, f32),
        ),
        grid_spec=pltpu.PrefetchScalarGridSpec(
            num_scalar_prefetch=1,
            grid=(matrices * heads,),
            in_specs=[
                block,
                block,
                pl.BlockSpec((1, head, rank), lambda i, owners: (i // heads, i % heads, 0)),
                pl.BlockSpec((1, rank, width), lambda i, owners: (i // heads, 0, 0)),
                fixed(matrices, 8, width),
                mats,
                mats,
                vecs,
                vecs,
            ],
            out_specs=(block, mats, mats, vecs, vecs),
        ),
        name="apply",
    )(owners, grads, errors, p_hat, q_factor, vec_avg, mat_momentum, mat_weights, vec_momentum, vec_weights)


def solution(mesh):
    both = ("rep", "grp")
    placed = (
        P(both, None, None, None), P(both, None, None, None), P(), P(both, None, None), P(),
        P(both, None, None), P(both, None, None), P(both, None), P(both, None),
    )
    return jax.shard_map(
        local,
        mesh=mesh,
        in_specs=placed,
        out_specs=(P(both, None, None, None), P(both, None, None), P(both, None, None), P(both, None), P(both, None)),
        check_vma=False,
    )
```

```python
import functools

import jax
import jax.numpy as jnp
from jax import lax
from jax.experimental import pallas as pl
from jax.experimental.pallas import tpu as pltpu
from jax.sharding import PartitionSpec as P

ROOT_ITERS = 12
MESH = pl.DeviceIdType.MESH
HIGH = lax.Precision.HIGHEST
PARTS = 6
SPLITS = 4
SUBS = (32, 24)
STEPS = 2 * SPLITS + 2
CHUNK = 64


def dot(a, b, dims=((1,), (0,))):
    return lax.dot_general(a, b, (dims, ((), ())), precision=HIGH, preferred_element_type=jnp.float32)


def split(value):
    coarse = value.astype(jnp.bfloat16)
    return coarse, (value - coarse.astype(jnp.float32)).astype(jnp.bfloat16)


def split_dot(a, b, dims=((1,), (0,))):
    def one(left, right):
        return lax.dot_general(left, right, (dims, ((), ())), preferred_element_type=jnp.float32)

    coarse, fine = split(a)
    both = one(jnp.concatenate([coarse, fine], axis=0), b[0])
    return both[: a.shape[0]] + (both[a.shape[0] :] + one(coarse, b[1]))


def orthonormal(factor):
    rank = factor.shape[0]
    gram = dot(factor, factor, ((1,), (1,)))
    spread = jnp.sqrt(jnp.sum(gram * gram, keepdims=True))
    row = lax.broadcasted_iota(jnp.int32, (rank, rank), 0)
    column = lax.broadcasted_iota(jnp.int32, (rank, rank), 1)
    identity = jnp.where(row == column, 1.0, 0.0).astype(jnp.float32)
    left = gram / spread
    middle = 1.5 * identity - 0.5 * left
    left = dot(left, middle)
    right = middle
    for sweep in range(1, ROOT_ITERS):
        middle = 1.5 * identity - 0.5 * dot(right, left)
        if sweep < ROOT_ITERS - 1:
            left = dot(left, middle)
        right = dot(middle, right)
    return dot(right, factor, ((0,), (0,))) / jnp.sqrt(spread)


def reduce_kernel(grads_ref, errors_ref, warm_ref, vec_ref, q_out, p_out, v_out, *scratch):
    halves = scratch[:SPLITS]
    (
        grads, errors, away, pair, mine, whole0, whole1, middle, total, p_sums, p_recv, q_mine, q_pair, p_mine, p_pair,
        v_pair, load_sem, pair_sem, step_send, step_recv, p_sem, last_sem,
    ) = scratch[SPLITS:]
    core = lax.axis_index("rep") % 2
    place = (lax.axis_index("rep") // 8, (lax.axis_index("rep") // 2) % 4, lax.axis_index("grp"))
    rows, width = errors_ref.shape[2], errors_ref.shape[3]
    high = mine.shape[0]
    tail = high - rows
    count = lax.axis_size("rep") * lax.axis_size("grp")

    def device(x, y, z, c):
        return ((x * 4 + y) * 2 + c, z)

    bits, peers = [], []
    for kind in range(2):
        for axis in range(3):
            at = place[axis]
            moved = list(place)
            moved[axis] = at + 1 - 2 * (at % 2) if kind == 0 else 3 - at
            peers.append(device(*moved, core))
            bits.append((at + at // 2) % 2 if kind == 0 else at // 2)
    partner = device(*place, 1 - core)

    def remote(src, dst, send_sem, recv_sem, to):
        copy = pltpu.make_async_remote_copy(
            src_ref=src, dst_ref=dst, send_sem=send_sem, recv_sem=recv_sem, device_id=to, device_id_type=MESH
        )
        copy.start()
        return copy

    loads = {}
    starts = list(range(0, rows, CHUNK))
    for turn in range(2):
        matrix = 1 - core if turn == 0 else core
        for number, start in enumerate(starts):
            window = pl.ds(start, CHUNK)
            slot = turn * len(starts) + number
            loads[turn, number] = (
                pltpu.make_async_copy(grads_ref.at[0, matrix, window], grads.at[turn, window], load_sem.at[0, slot]),
                pltpu.make_async_copy(errors_ref.at[0, matrix, window], errors.at[turn, window], load_sem.at[1, slot]),
            )
            for copy in loads[turn, number]:
                copy.start()

    barrier = pltpu.get_barrier_semaphore()
    for peer in peers + [partner]:
        pl.semaphore_signal(barrier, inc=1, device_id=peer, device_id_type=MESH)

    first_row = lax.broadcasted_iota(jnp.int32, (tail, width), 0) == 0
    away[rows:, :] = jnp.where(first_row, vec_ref[0, pl.ds(1 - core, 1), :], 0.0)
    mine[rows:, :] = jnp.where(first_row, vec_ref[0, pl.ds(core, 1), :], 0.0)
    pl.semaphore_wait(barrier, len(peers) + 1)

    def combine(turn, number, into):
        for copy in loads[turn, number]:
            copy.wait()
        window = pl.ds(starts[number], CHUNK)
        into[window, :] = grads[turn, window, :].astype(jnp.float32) + errors[turn, window, :]

    sent = []
    handed = []
    for number, start in enumerate(starts):
        combine(0, number, away)
        window = pl.ds(start, CHUNK if number < len(starts) - 1 else CHUNK + tail)
        copy = remote(away.at[window], pair.at[window], pair_sem.at[0, number], pair_sem.at[1, number], partner)
        handed.append(copy)
        sent.append(copy)

    pieces = []
    for sub, size in enumerate(SUBS):
        for part in range(PARTS):
            pieces.append((part, PARTS * sum(SUBS[:sub]) + part * size, size))
    offsets = []
    for part in range(PARTS):
        chain = [0]
        for step in range(SPLITS):
            chain.append(chain[-1] + bits[(part + step) % 6] * (width >> (step + 1)))
        offsets.append(chain)

    def columns(part, depth):
        return pl.ds(pl.multiple_of(offsets[part][depth], 128), width >> depth)

    def others(part, depth):
        half = width >> depth
        begin = offsets[part][depth - 1] + (1 - bits[(part + depth - 1) % 6]) * half
        return pl.ds(pl.multiple_of(begin, 128), half)

    flight = {}

    def begin(step, number):
        part, start, size = pieces[number]
        window = pl.ds(start, size)
        link = (part + (step if step < SPLITS + 2 else STEPS - 1 - step)) % 6
        if step < SPLITS:
            src, dst = mine.at[window, others(part, step + 1)], halves[step].at[window]
        elif step == SPLITS:
            src, dst = mine.at[window, columns(part, SPLITS)], whole0.at[window]
        elif step == SPLITS + 1:
            src, dst = middle.at[window], whole1.at[window]
        else:
            src = dst = total.at[window, columns(part, STEPS - step)]
        flight[step, number] = remote(
            src, dst, step_send.at[step, number], step_recv.at[step, number], peers[link]
        )
        sent.append(flight[step, number])

    def finish(step, number):
        part, start, size = pieces[number]
        window = pl.ds(start, size)
        flight[step, number].wait_recv()
        if step < SPLITS:
            cols = columns(part, step + 1)
            mine[window, cols] = mine[window, cols] + halves[step][window, :]
        elif step == SPLITS:
            middle[window, :] = mine[window, columns(part, SPLITS)] + whole0[window, :]
        elif step == SPLITS + 1:
            total[window, columns(part, SPLITS)] = middle[window, :] + whole1[window, :]

    for number in range(len(starts)):
        combine(1, number, mine)
    for number, start in enumerate(starts):
        handed[number].wait_recv()
        size = CHUNK if number < len(starts) - 1 else CHUNK + tail
        window = pl.ds(start, size)
        mine[window, :] = mine[window, :] + pair[window, :]
        for piece, (part, first, extent) in enumerate(pieces):
            if start < first + extent <= start + size:
                begin(0, piece)

    rank = warm_ref.shape[1]
    live = lax.broadcasted_iota(jnp.int32, (rank, high), 1) < rows
    p_sums[0] = jnp.where(live, split_dot(warm_ref[core], split(mine[...]), ((1,), (1,))), 0.0)
    p_flight = None
    for step in range(STEPS):
        if step < 6:
            p_flight = remote(p_sums.at[step], p_recv.at[step], p_sem.at[0, step], p_sem.at[1, step], peers[step])
            sent.append(p_flight)
        for number in range(len(pieces)):
            finish(step, number)
            if step < STEPS - 1:
                begin(step + 1, number)
        if step < 6:
            p_flight.wait_recv()
            p_sums[step + 1] = p_sums[step] + p_recv[step]
        if step == STEPS - 2:
            p_hat = orthonormal(p_sums[6] / count)
    v_copy = remote(total.at[pl.ds(rows, 8)], v_pair, last_sem.at[0, 0], last_sem.at[1, 0], partner)
    parts = split(total[...])
    q_factor = split_dot(p_hat, parts) / count
    p_sum = jnp.where(live, split_dot(q_factor, parts, ((1,), (1,))), 0.0)
    p_hat = orthonormal(p_sum / count)
    p_mine[...] = p_hat
    p_copy = remote(p_mine, p_pair, last_sem.at[0, 1], last_sem.at[1, 1], partner)
    q_mine[...] = split_dot(p_hat, parts) / count
    q_copy = remote(q_mine, q_pair, last_sem.at[0, 2], last_sem.at[1, 2], partner)
    v_out[core] = total[rows : rows + 8, :] / count
    p_out[core] = p_mine[...].T[:rows]
    q_out[core] = q_mine[...]
    v_copy.wait_recv()
    v_out[1 - core] = v_pair[...] / count
    p_copy.wait_recv()
    p_out[1 - core] = p_pair[...].T[:rows]
    q_copy.wait_recv()
    q_out[1 - core] = q_pair[...]
    for copy in sent + [v_copy, p_copy, q_copy]:
        copy.wait_send()


def apply_kernel(
    owners, grads, errors, p_hat, q_factor, vec_avg, mat_m, mat_w, vec_m, vec_w,
    new_errors, mat_m_out, mat_w_out, vec_m_out, vec_w_out,
):
    step = pl.program_id(0)
    device = lax.axis_index("rep") * lax.axis_size("grp") + lax.axis_index("grp")
    items = owners.shape[0]
    heads = items - vec_m.shape[0]

    def home(item):
        owner = owners[item]
        slot = jnp.int32(0)
        for before in range(items):
            slot += jnp.where((before < item) & (owners[before] == owner), 1, 0)
        return owner == device, slot

    @pl.when(step == 0)
    def _():
        mat_m_out[...] = mat_m[...]
        mat_w_out[...] = mat_w[...]
        vec_m_out[...] = vec_m[...]
        vec_w_out[...] = vec_w[...]
        for gain in range(items - heads):
            here, slot = home(heads + gain)

            @pl.when(here)
            def _():
                moment = 0.9 * vec_m[pl.ds(slot, 1), :] + vec_avg[gain, :1, :]
                vec_m_out[pl.ds(slot, 1), :] = moment
                vec_w_out[pl.ds(slot, 1), :] = vec_w[pl.ds(slot, 1), :] - 0.5 * moment

    approx = split_dot(p_hat[0], split(q_factor[0]))
    new_errors[0, 0] = grads[0, 0].astype(jnp.float32) + errors[0, 0] - approx
    here, slot = home(step)

    @pl.when(here)
    def _():
        moment = 0.9 * mat_m[slot] + approx
        mat_m_out[slot] = moment
        mat_w_out[slot] = mat_w[slot] - 0.5 * moment


def local(grads, errors, warm_start, vec_grads, owners, mat_momentum, mat_weights, vec_momentum, vec_weights):
    _, matrices, rows, width = errors.shape
    rank = warm_start.shape[1]
    high = PARTS * sum(SUBS)
    f32 = jnp.float32
    pieces = PARTS * len(SUBS)
    vmem = pl.BlockSpec(memory_space=pltpu.VMEM)
    hbm = pl.BlockSpec(memory_space=pl.ANY)
    dma = pltpu.SemaphoreType.DMA
    q_factor, p_hat, vec_avg = pl.pallas_call(
        reduce_kernel,
        out_shape=(
            jax.ShapeDtypeStruct((matrices, rank, width), f32),
            jax.ShapeDtypeStruct((matrices, rows, rank), f32),
            jax.ShapeDtypeStruct((matrices, 8, width), f32),
        ),
        in_specs=[hbm, hbm, vmem, vmem],
        out_specs=(vmem, vmem, vmem),
        scratch_shapes=[pltpu.VMEM((high, width >> (step + 1)), f32) for step in range(SPLITS)]
        + [
            pltpu.VMEM((2, rows, width), jnp.bfloat16),
            pltpu.VMEM((2, rows, width), f32),
            pltpu.VMEM((high, width), f32),
            pltpu.VMEM((high, width), f32),
            pltpu.VMEM((high, width), f32),
            pltpu.VMEM((high, width >> SPLITS), f32),
            pltpu.VMEM((high, width >> SPLITS), f32),
            pltpu.VMEM((high, width >> SPLITS), f32),
            pltpu.VMEM((high, width), f32),
            pltpu.VMEM((7, rank, high), f32),
            pltpu.VMEM((6, rank, high), f32),
            pltpu.VMEM((rank, width), f32),
            pltpu.VMEM((rank, width), f32),
            pltpu.VMEM((rank, high), f32),
            pltpu.VMEM((rank, high), f32),
            pltpu.VMEM((8, width), f32),
            dma((2, 2 * (rows // CHUNK))),
            dma((2, rows // CHUNK)),
            dma((STEPS, pieces)),
            dma((STEPS, pieces)),
            dma((2, 6)),
            dma((2, 3)),
        ],
        compiler_params=pltpu.CompilerParams(
            collective_id=0, has_side_effects=True, vmem_limit_bytes=60 * 1024 * 1024
        ),
        name="reduce",
    )(grads, errors, warm_start, vec_grads)

    heads = rows // mat_momentum.shape[1]
    head = mat_momentum.shape[1]
    slots = mat_momentum.shape[0]
    block = pl.BlockSpec((1, 1, head, width), lambda i, owners: (0, i // heads, i % heads, 0))

    def fixed(*shape):
        return pl.BlockSpec(shape, lambda i, owners: (0,) * len(shape))

    mats, vecs = fixed(slots, head, width), fixed(slots, width)
    return pl.pallas_call(
        apply_kernel,
        out_shape=(
            jax.ShapeDtypeStruct(errors.shape, f32),
            jax.ShapeDtypeStruct(mat_momentum.shape, f32),
            jax.ShapeDtypeStruct(mat_weights.shape, f32),
            jax.ShapeDtypeStruct(vec_momentum.shape, f32),
            jax.ShapeDtypeStruct(vec_weights.shape, f32),
        ),
        grid_spec=pltpu.PrefetchScalarGridSpec(
            num_scalar_prefetch=1,
            grid=(matrices * heads,),
            in_specs=[
                block,
                block,
                pl.BlockSpec((1, head, rank), lambda i, owners: (i // heads, i % heads, 0)),
                pl.BlockSpec((1, rank, width), lambda i, owners: (i // heads, 0, 0)),
                fixed(matrices, 8, width),
                mats,
                mats,
                vecs,
                vecs,
            ],
            out_specs=(block, mats, mats, vecs, vecs),
        ),
        name="apply",
    )(owners, grads, errors, p_hat, q_factor, vec_avg, mat_momentum, mat_weights, vec_momentum, vec_weights)


def solution(mesh):
    both = ("rep", "grp")
    placed = (
        P(both, None, None, None), P(both, None, None, None), P(), P(both, None, None), P(),
        P(both, None, None), P(both, None, None), P(both, None), P(both, None),
    )
    return jax.shard_map(
        local,
        mesh=mesh,
        in_specs=placed,
        out_specs=(P(both, None, None, None), P(both, None, None), P(both, None, None), P(both, None), P(both, None)),
        check_vma=False,
    )
```
